32 devices in a mesh: space: 8 (over y, x, core), member: 4 (over z).
Axes of the slice: x: 2, y: 2, z: 4, core: 2. Of those that a mesh axis runs over, the one named last changes fastest.
Arguments:
- obs_pert: bfloat16 [80, 16384], P('member', 'space'), may hold values from -6 to 6
- innovation: bfloat16 [16384], P('space'), may hold values from -6 to 6
- obs_prec: bfloat16 [16384], P('space'), may hold values from 1 to 100
- obs_lists: int32 [1536, 256], P('space'), may hold values from 0 to 6143
- loc_weight: bfloat16 [1536, 256], P('space'), may hold values from 0.049804688 to 1
- send_rows: int32 [8, 4, 8], P('space'), may hold values from 0 to 47
- ocean_src: int32 [48, 2], P('space'), may hold values from 0 to 31, as said below
- ocean_frac: float32 [48], P('space'), may hold values from 0 to 1
- ocean_ens: bfloat16 [80, 48, 2048], P(None, 'space', 'member'), may hold values from -6 to 6
Outputs:
- ocean_anal: bfloat16 [80, 48, 2048], P(None, 'space', 'member')
The draws below stay inside these ranges and needn't reach their ends.
Inputs may be any that keep to these rules, and one draw needn't show every extreme that they name: `ocean_src`: the two slots of one ocean block differ.
All inputs are finite; a program needn't handle non-finite values.
Results may differ from the reference program's by a relative error of at most 0.0064.
Values may be sent and summed in bfloat16 or wider, within the bound.
A program may use at most 64 MiB of HBM per device.

```python
import math
import jax
import jax.numpy as jnp
from jax import lax

K = 80
OBS_DEV = 2048
LOBS = 256
ABLK_TILE = 192
ITERS = 12
OB_TILE = 6
GROUP = 48
OCELLS = 2048
NOBS = 16384
ABLK = 1536
OBLK = 48
N_SPACE = 8
N_MEMBER = 4
DEVICES = 32


def draw_ocean_src(key, part):

    def one_tile(tile_key):
        key_perm, key_order = jax.random.split(tile_key)
        shuffled = jax.random.permutation(key_perm, DEVICES)
        order = jax.random.permutation(key_order, 2 * OB_TILE)
        values = shuffled[order % DEVICES]
        return values.reshape(OB_TILE, 2)
    tile_keys = jax.random.split(jax.random.fold_in(key, 7), N_SPACE)
    return jax.vmap(one_tile)(tile_keys).reshape(OB_TILE * N_SPACE, 2).astype(jnp.int32)


def touch_ends(result, stream_key, smallest, largest):
    longest = result.shape.index(max(result.shape))
    spots = []
    for shift in (0, 1):
        where = [jax.random.randint(jax.random.fold_in(stream_key, axis), (), 0, length) for axis, length in enumerate(result.shape)]
        where[longest] = (where[longest] + shift) % result.shape[longest]
        spots.append(tuple(where))
    return result.at[spots[0]].set(smallest).at[spots[1]].set(largest)


def steps_of(stream_key, dims, shards, low, high):
    loudness, own = 1.0, jax.random.fold_in(stream_key, 6)
    for position, blocks in shards:
        draws = jnp.exp(jax.random.uniform(jax.random.fold_in(own, position), (blocks,), jnp.float32, low / len(shards), high / len(shards)))
        loudness = loudness * jnp.repeat(draws, dims[position] // blocks).reshape([-1 if axis == position else 1 for axis in range(len(dims))])
    return loudness


def noise(rng, shape, scale, reach, pieces=(), kind=jnp.bfloat16):
    result = scale * jax.random.normal(rng, shape, jnp.float32)
    if pieces:
        result = result * steps_of(rng, shape, pieces, -0.22, 0.18)
    return jnp.clip(result, -reach, reach).astype(kind)


def setup_inputs(seed: int = 0) -> dict:
    keys = jax.random.split(jax.random.key(seed), 10)
    return {
        "obs_pert": noise(keys[0], (K, NOBS), 1.0, 6.0, ((0, 4), (1, 8))),
        "innovation": noise(keys[1], (NOBS,), 1.0, 6.0, ((0, 8),)),
        "obs_prec": jnp.clip(jnp.exp(math.log(100.0) - 4.6051702 * jax.random.uniform(keys[2], (NOBS,), jnp.float32) ** steps_of(keys[2], (NOBS,), ((0, 8),), -0.2, 0.2)), 1.0, 100.0).astype(jnp.bfloat16),
        "obs_lists": touch_ends(jax.random.randint(keys[3], (ABLK, LOBS), 0, 3 * OBS_DEV), jax.random.fold_in(keys[3], 1), 0, (3 * OBS_DEV) - 1).astype(jnp.int32),
        "loc_weight": jnp.clip(0.049804688 + 0.9501953 * jax.random.uniform(keys[4], (ABLK, LOBS), jnp.float32) ** steps_of(keys[4], (ABLK, LOBS), ((0, 8),), -0.2, 0.2), 0.049804688, 1.0).astype(jnp.bfloat16),
        "send_rows": touch_ends(jax.random.randint(keys[5], (N_SPACE, N_MEMBER, N_SPACE), 0, GROUP), jax.random.fold_in(keys[5], 1), 0, GROUP - 1).astype(jnp.int32),
        "ocean_src": draw_ocean_src(jax.random.fold_in(keys[9], 71), 0),
        "ocean_frac": jnp.clip(1.0 * jax.random.uniform(keys[7], (OBLK,), jnp.float32) ** steps_of(keys[7], (OBLK,), ((0, 8),), -0.2, 0.2), 0.0, 1.0),
        "ocean_ens": noise(keys[8], (K, OBLK, OCELLS), 1.0, 6.0, ((1, 8), (2, 4))),
    }


def transform(local_obs, loc_sel, innov_sel, prec_sel):
    members = local_obs.shape[0]
    obs_f32 = local_obs.astype(jnp.float32)
    obs_weight = loc_sel.astype(jnp.float32) * prec_sel.astype(jnp.float32)
    weighted = obs_f32 * obs_weight[None]
    gram = jnp.einsum('ibl,jbl->bij', weighted, obs_f32, precision=lax.Precision.HIGHEST)
    pulled = jnp.einsum('ibl,bl->bi', weighted, innov_sel.astype(jnp.float32), precision=lax.Precision.HIGHEST)
    identity = jnp.eye(members, dtype=jnp.float32)
    precision_mat = (members - 1.0) * identity + gram
    scale_sum = jnp.trace(precision_mat, axis1=1, axis2=2)
    root_start = precision_mat / scale_sum[:, None, None]
    inverse_start = jnp.broadcast_to(identity, precision_mat.shape)

    def newton(iteration, carry):
        root_iter, inverse_iter = carry
        correction = 1.5 * identity - 0.5 * jnp.einsum('bij,bjk->bik', inverse_iter, root_iter, precision=lax.Precision.HIGHEST)
        root_next = jnp.einsum('bij,bjk->bik', root_iter, correction, precision=lax.Precision.HIGHEST)
        inverse_next = jnp.einsum('bij,bjk->bik', correction, inverse_iter, precision=lax.Precision.HIGHEST)
        return (root_next, inverse_next)
    root_iter, inverse_iter = lax.fori_loop(0, ITERS, newton, (root_start, inverse_start))
    spread = jnp.sqrt((members - 1.0) / scale_sum)[:, None, None] * inverse_iter
    half_way = jnp.einsum('bij,bj->bi', inverse_iter, pulled, precision=lax.Precision.HIGHEST)
    mean_weight = jnp.einsum('bij,bj->bi', inverse_iter, half_way, precision=lax.Precision.HIGHEST) / scale_sum[:, None]
    return (spread + mean_weight[:, :, None]).astype(jnp.bfloat16)

def apply_weights(ensemble, trans_one, trans_two, frac):
    frac_col = frac[:, None, None]
    mixed = ((1.0 - frac_col) * trans_one.astype(jnp.float32) + frac_col * trans_two.astype(jnp.float32)).astype(jnp.bfloat16)
    ens_f32 = ensemble.astype(jnp.float32)
    ens_mean = lax.optimization_barrier(jnp.mean(ens_f32, axis=0))
    deviation = (ens_f32 - ens_mean[None]).astype(jnp.bfloat16)
    product = jnp.einsum('jol,oji->iol', deviation.astype(jnp.float32), mixed.astype(jnp.float32))
    return (ens_mean[None] + product).astype(jnp.bfloat16)

def reference(obs_pert, innovation, obs_prec, obs_lists, loc_weight, send_rows, ocean_src, ocean_frac, ocean_ens):
    group_len = ABLK_TILE // N_MEMBER
    total_obs = obs_pert.shape[1]

    def one_tile(tile_idx):
        sources = lax.dynamic_slice_in_dim(ocean_src, tile_idx * OB_TILE, OB_TILE, 0).reshape(-1)
        member_part = sources // N_SPACE
        space_part = sources % N_SPACE
        local_row = send_rows[space_part, member_part, tile_idx]
        block_ids = (space_part * ABLK_TILE + member_part * group_len + local_row).astype(jnp.int32)
        lists = obs_lists[block_ids]
        offsets = (space_part - 1) * OBS_DEV
        global_idx = ((lists + offsets[:, None]) % total_obs).astype(jnp.int32)
        local_obs = obs_pert[:, global_idx]
        weights = transform(local_obs, loc_weight[block_ids], innovation[global_idx], obs_prec[global_idx])
        weights = weights.reshape(OB_TILE, 2, K, K)
        ensemble = lax.dynamic_slice_in_dim(ocean_ens, tile_idx * OB_TILE, OB_TILE, 1)
        frac = lax.dynamic_slice_in_dim(ocean_frac, tile_idx * OB_TILE, OB_TILE, 0)
        return apply_weights(ensemble, weights[:, 0], weights[:, 1], frac)
    tiles = lax.map(one_tile, jnp.arange(N_SPACE, dtype=jnp.int32))
    return jnp.moveaxis(tiles, 0, 1).reshape(K, OB_TILE * N_SPACE, OCELLS)
```

```python
import functools

import jax
import jax.numpy as jnp
from jax import lax
from jax.experimental import pallas as pl
from jax.experimental.pallas import tpu as pltpu
from jax.sharding import PartitionSpec as P

ITERS = 12
LANES = 128
CHUNK = 512


def split(value):
    high = value.astype(jnp.bfloat16)
    low = (value - high.astype(jnp.float32)).astype(jnp.bfloat16)
    return high, low


def left_side(value):
    return jnp.concatenate(split(value), axis=1)


def right_side(value):
    pair = left_side(value)
    filler = jnp.zeros((LANES - pair.shape[0], pair.shape[1]), jnp.bfloat16)
    return jnp.concatenate([pair, filler, pair, filler], axis=0)


def halves(product):
    return product[:, :LANES] + product[:, LANES:]


def mm(lhs, rhs):
    return jnp.dot(lhs, rhs, preferred_element_type=jnp.float32)


def transform_kernel(
    group, members, send_ref, lists_ref, loc_ref, left_ref, mid_ref, right_ref, prec_ref, out_ref,
    loc_f32, dense, gram, root, inverse, pulled, scales,
):
    member_idx = lax.axis_index("member")
    n_member = send_ref.shape[0]
    group_len = lists_ref.shape[0] // n_member
    first = pl.program_id(0) * group
    loc_f32[...] = loc_ref[...].astype(jnp.float32)
    his = dense.shape[1]
    lobs = lists_ref.shape[1]
    hi_iota = lax.broadcasted_iota(jnp.int32, (his, lobs), 0)
    lo_iota = lax.broadcasted_iota(jnp.int32, (LANES, lobs), 0)
    for b in range(group):
        row = send_ref[member_idx, first + b] + member_idx * group_len
        spots = lists_ref[pl.ds(row, 1), :]
        taper = loc_f32[pl.ds(row, 1), :]
        hi_hot = jnp.where(hi_iota == spots // LANES, taper, 0.0).astype(jnp.bfloat16)
        lo_hot = jnp.where(lo_iota == spots % LANES, 1.0, 0.0).astype(jnp.bfloat16)
        dense[b] = prec_ref[...] * lax.dot_general(
            hi_hot, lo_hot, (((1,), (1,)), ((), ())), preferred_element_type=jnp.float32
        )
    gram[...] = jnp.zeros_like(gram)
    per = CHUNK // LANES
    for piece, ref in enumerate((left_ref, mid_ref, right_ref)):
        tile_obs = ref.shape[1]

        def chunk_step(c, carry, ref=ref, base=piece * (tile_obs // LANES)):
            cells = ref[:, pl.ds(pl.multiple_of(c * CHUNK, CHUNK), CHUNK)]
            wide = cells[:members].astype(jnp.float32)
            highs, lows = [], []
            for b in range(group):
                parts = []
                for j in range(per):
                    weight = dense[b, pl.ds(base + c * per + j, 1), :]
                    parts.append(wide[:, j * LANES : (j + 1) * LANES] * weight)
                high, low = split(jnp.concatenate(parts, axis=1))
                highs.append(high)
                lows.append(low)
            rhs = (((1,), (1,)), ((), ()))
            for b in range(group):
                both = lax.dot_general(
                    highs[b], cells, rhs, preferred_element_type=jnp.float32
                ) + lax.dot_general(lows[b], cells, rhs, preferred_element_type=jnp.float32)
                gram[b, :, : cells.shape[0]] += both
            return carry

        lax.fori_loop(0, tile_obs // CHUNK, chunk_step, 0)

    rows = lax.broadcasted_iota(jnp.int32, (members, LANES), 0)
    cols = lax.broadcasted_iota(jnp.int32, (members, LANES), 1)
    on_diag = rows == cols
    half3 = jnp.where(on_diag, 1.5, 0.0)
    for b in range(group):
        both = gram[b]
        pulled[b] = jnp.sum(jnp.where(cols == members, both, 0.0), axis=1, keepdims=True)
        matrix = jnp.where(cols < members, both, 0.0) + jnp.where(on_diag, members - 1.0, 0.0)
        scale = jnp.sum(
            jnp.sum(jnp.where(on_diag, matrix, 0.0), axis=1, keepdims=True), axis=0, keepdims=True
        )
        scales[b] = jnp.broadcast_to(scale, (1, LANES))
        start = matrix / scale
        correction = half3 - 0.5 * start
        root[b] = halves(mm(left_side(start), right_side(correction)))
        inverse[b] = correction

    def newton(step, carry):
        corrections = []
        roots, inverses = [], []
        for b in range(group):
            roots.append(left_side(root[b]))
            inverses.append(left_side(inverse[b]))
            filler = jnp.zeros((LANES - members, 2 * LANES), jnp.bfloat16)
            rhs = jnp.concatenate([roots[b], filler, roots[b], filler], axis=0)
            corrections.append(half3 - 0.5 * halves(mm(inverses[b], rhs)))
        for b in range(group):
            both = halves(
                mm(jnp.concatenate([roots[b], inverses[b]], axis=0), right_side(corrections[b]))
            )
            root[b] = both[:members]
            inverse[b] = both[members:]
        return carry

    lax.fori_loop(0, ITERS - 1, newton, 0)

    for b in range(group):
        z = inverse[b]
        scale = scales[b]
        half_way = jnp.sum(z * pulled[b], axis=0, keepdims=True)
        mean_weight = jnp.sum(z * half_way, axis=1, keepdims=True) / scale[:, :1]
        trans = jnp.sqrt((members - 1.0) / scale) * z + mean_weight
        out_ref[b] = trans[:, :members].astype(jnp.bfloat16)


def transforms(send, lists, loc, left, mid, right, prec, count):
    members = left.shape[0] - 16
    group = 8 if count % 8 == 0 else count
    his = prec.shape[0]
    full = lambda a: pl.BlockSpec(a.shape, lambda i, n=a.ndim: (0,) * n)
    return pl.pallas_call(
        functools.partial(transform_kernel, group, members),
        grid=(count // group,),
        in_specs=[pl.BlockSpec(memory_space=pltpu.SMEM)]
        + [full(a) for a in (lists, loc, left, mid, right, prec)],
        out_specs=pl.BlockSpec((group, members, members), lambda i: (i, 0, 0)),
        out_shape=jax.ShapeDtypeStruct((count, members, members), jnp.bfloat16),
        scratch_shapes=[
            pltpu.VMEM(loc.shape, jnp.float32),
            pltpu.VMEM((group, his, LANES), jnp.float32),
            pltpu.VMEM((group, members, LANES), jnp.float32),
            pltpu.VMEM((group, members, LANES), jnp.float32),
            pltpu.VMEM((group, members, LANES), jnp.float32),
            pltpu.VMEM((group, members, 1), jnp.float32),
            pltpu.VMEM((group, 1, LANES), jnp.float32),
        ],
        name="transforms",
    )(send, lists, loc, left, mid, right, prec)


def shift(cells, by):
    count = lax.axis_size("space")
    return lax.ppermute(cells, "space", [(i, (i + by) % count) for i in range(count)])


def mix_pair(trans_one, trans_two, frac):
    frac_col = frac[:, None, None]
    return (
        (1.0 - frac_col) * trans_one.astype(jnp.float32) + frac_col * trans_two.astype(jnp.float32)
    ).astype(jnp.bfloat16)


def apply_weights(ensemble, mixed):
    ens_mean = jnp.mean(ensemble, axis=0, dtype=jnp.float32)
    deviation = (ensemble.astype(jnp.float32) - ens_mean[None]).astype(jnp.bfloat16)
    product = jnp.einsum("jol,oji->iol", deviation, mixed, preferred_element_type=jnp.float32)
    return (ens_mean[None] + product).astype(jnp.bfloat16)


def shards(
    obs_pert,
    innovation,
    obs_prec,
    obs_lists,
    loc_weight,
    send_rows,
    ocean_src,
    ocean_frac,
    ocean_ens,
):
    n_space = lax.axis_size("space")
    tile_obs = obs_pert.shape[1]
    members = lax.all_gather(obs_pert, "member", axis=0, tiled=True)
    extra = jnp.zeros((16, tile_obs), jnp.bfloat16).at[0].set(innovation).at[1].set(obs_prec)
    mid = jnp.concatenate([members, extra], axis=0)
    left, right = shift(mid, 1), shift(mid, -1)
    k = members.shape[0]
    prec = jnp.stack([left[k + 1], obs_prec, right[k + 1]]).astype(jnp.float32)
    prec = prec.reshape(-1, LANES)
    weights = transforms(send_rows[0], obs_lists, loc_weight, left, mid, right, prec, n_space)
    arrived = lax.all_to_all(weights, "space", split_axis=0, concat_axis=0, tiled=True)
    weight_table = lax.all_gather(arrived, "member", axis=0, tiled=True)
    mixed = mix_pair(weight_table[ocean_src[:, 0]], weight_table[ocean_src[:, 1]], ocean_frac)
    return apply_weights(ocean_ens, mixed)


def solution(mesh):
    return jax.shard_map(
        shards,
        mesh=mesh,
        in_specs=(
            P("member", "space"),
            P("space"),
            P("space"),
            P("space", None),
            P("space", None),
            P("space", None, None),
            P("space", None),
            P("space"),
            P(None, "space", "member"),
        ),
        out_specs=P(None, "space", "member"),
        check_vma=False,
    )
```

```python
import functools

import jax
import jax.numpy as jnp
from jax import lax
from jax.experimental import pallas as pl
from jax.experimental.pallas import tpu as pltpu
from jax.sharding import PartitionSpec as P

ITERS = 12
LANES = 128
CHUNK = 512


def split(value):
    high = value.astype(jnp.bfloat16)
    low = (value - high.astype(jnp.float32)).astype(jnp.bfloat16)
    return high, low


def left_side(value):
    return jnp.concatenate(split(value), axis=1)


def right_side(value):
    pair = left_side(value)
    filler = jnp.zeros((LANES - pair.shape[0], pair.shape[1]), jnp.bfloat16)
    return jnp.concatenate([pair, filler, pair, filler], axis=0)


def halves(product):
    return product[:, :LANES] + product[:, LANES:]


def mm(lhs, rhs):
    return jnp.dot(lhs, rhs, preferred_element_type=jnp.float32)


MESH = pl.DeviceIdType.MESH


def remote(src, dst, send_sem, recv_sem, device):
    return pltpu.make_async_remote_copy(
        src_ref=src, dst_ref=dst, send_sem=send_sem, recv_sem=recv_sem,
        device_id=device, device_id_type=MESH,
    )


def letkf_kernel(
    group, ns, nm,
    send_ref, coef_ref, lists_ref, loc_ref, pert_ref, extra_ref, out_ref,
    pert_all, extra_all, loc_f32, dense, gram, root, inverse, pulled, scales,
    trans_out, trans_in, up_out, up_in, down_out, down_in, mixed,
    z_send, z_recv, near_send, near_recv, info_send, info_recv, t_send, t_recv,
    up_send, up_recv, down_send, down_recv,
):
    s = lax.axis_index("space")
    m = lax.axis_index("member")
    members = pert_ref.shape[0] * nm
    tile_obs = pert_ref.shape[1]
    tile_his = tile_obs // LANES
    group_len = lists_ref.shape[0] // nm
    oblocks = out_ref.shape[0]
    z_peers = [lax.rem(m + k, nm) for k in range(1, nm)]
    s_peers = [lax.rem(s + k, ns) for k in range(1, ns)]
    left, right = lax.rem(s + ns - 1, ns), lax.rem(s + 1, ns)

    barrier = pltpu.get_barrier_semaphore()
    for peer in z_peers:
        pl.semaphore_signal(barrier, inc=1, device_id=(s, peer), device_id_type=MESH)
    for peer in s_peers:
        pl.semaphore_signal(barrier, inc=1, device_id=(peer, m), device_id_type=MESH)
    pl.semaphore_wait(barrier, len(z_peers) + len(s_peers))

    def to_z(peer):
        return remote(pert_ref, pert_all.at[1, m], z_send.at[peer], z_recv.at[m], (s, peer))

    def from_z(peer):
        return remote(pert_ref, pert_all.at[1, peer], z_send.at[m], z_recv.at[peer], (s, peer))

    def near(side, owner, src):
        target = right if side == 0 else left
        return remote(
            src, pert_all.at[2 * side, owner], near_send.at[side, owner],
            near_recv.at[side, owner], (target, m),
        )

    def info(side):
        target = right if side == 0 else left
        return remote(
            extra_ref, extra_all.at[2 * side], info_send.at[side], info_recv.at[side], (target, m)
        )

    order = sorted(range(nm - 1), key=lambda k: abs(k + 1 - nm / 2))
    for k in order:
        to_z(z_peers[k]).start()
    for side in range(2):
        near(side, m, pert_ref).start()
        info(side).start()
    pert_all[1, m] = pert_ref[...]
    extra_all[1] = extra_ref[...]
    loc_f32[...] = loc_ref[...].astype(jnp.float32)

    his = dense.shape[1]
    lobs = lists_ref.shape[1]
    hi_iota = lax.broadcasted_iota(jnp.int32, (his, lobs), 0)
    lo_iota = lax.broadcasted_iota(jnp.int32, (LANES, lobs), 0)
    rows = lax.broadcasted_iota(jnp.int32, (members, LANES), 0)
    cols = lax.broadcasted_iota(jnp.int32, (members, LANES), 1)
    on_diag = rows == cols
    half3 = jnp.where(on_diag, 1.5, 0.0)
    per = CHUNK // LANES

    def spread_lists(first):
        for b in range(group):
            row = send_ref[m, first + b] + m * group_len
            spots = lists_ref[pl.ds(row, 1), :]
            taper = loc_f32[pl.ds(row, 1), :]
            high, low = lax.shift_right_logical(spots, 7), jnp.bitwise_and(spots, LANES - 1)
            hi_hot = jnp.where(hi_iota == high, taper, 0.0).astype(jnp.bfloat16)
            lo_hot = jnp.where(lo_iota == low, 1.0, 0.0).astype(jnp.bfloat16)
            dense[b] = lax.dot_general(
                hi_hot, lo_hot, (((1,), (1,)), ((), ())), preferred_element_type=jnp.float32
            )
        gram[...] = jnp.zeros_like(gram)

    def add_piece(piece):
        def chunk_step(c, carry):
            span = pl.ds(pl.multiple_of(c * CHUNK, CHUNK), CHUNK)
            wide = jnp.concatenate(
                [pert_all[piece, i, :, span].astype(jnp.float32) for i in range(nm)], axis=0
            )
            extra = extra_all[piece, :, span]
            cells = jnp.concatenate([wide.astype(jnp.bfloat16), extra], axis=0)
            wide = wide * extra.astype(jnp.float32)[1:2]
            contract = (((1,), (1,)), ((), ()))
            for b in range(group):
                parts = []
                for j in range(per):
                    weight = dense[b, pl.ds(piece * tile_his + c * per + j, 1), :]
                    parts.append(wide[:, j * LANES : (j + 1) * LANES] * weight)
                high, low = split(jnp.concatenate(parts, axis=1))
                gram[b, :, : cells.shape[0]] += lax.dot_general(
                    high, cells, contract, preferred_element_type=jnp.float32
                ) + lax.dot_general(low, cells, contract, preferred_element_type=jnp.float32)
            return carry

        lax.fori_loop(0, tile_obs // CHUNK, chunk_step, 0)

    def roots_and_weights(first):
        for b in range(group):
            both = gram[b]
            pulled[b] = jnp.sum(jnp.where(cols == members, both, 0.0), axis=1, keepdims=True)
            matrix = jnp.where(cols < members, both, 0.0) + jnp.where(on_diag, members - 1.0, 0.0)
            scale = jnp.sum(
                jnp.sum(jnp.where(on_diag, matrix, 0.0), axis=1, keepdims=True),
                axis=0, keepdims=True,
            )
            scales[b] = jnp.broadcast_to(scale, (1, LANES))
            start = matrix / scale
            correction = half3 - 0.5 * start
            root[b] = halves(mm(left_side(start), right_side(correction)))
            inverse[b] = correction

        def newton(step, carry):
            corrections, pairs = [], []
            filler = jnp.zeros((LANES - members, 2 * LANES), jnp.bfloat16)
            for b in range(group):
                r, z = left_side(root[b]), left_side(inverse[b])
                rhs = jnp.concatenate([r, filler, r, filler], axis=0)
                corrections.append(half3 - 0.5 * halves(mm(z, rhs)))
                pairs.append(jnp.concatenate([r, z], axis=0))
            for b in range(group):
                both = halves(mm(pairs[b], right_side(corrections[b])))
                root[b] = both[:members]
                inverse[b] = both[members:]
            return carry

        lax.fori_loop(0, ITERS - 1, newton, 0)
        for b in range(group):
            z = inverse[b]
            scale = scales[b]
            half_way = jnp.sum(z * pulled[b], axis=0, keepdims=True)
            mean_weight = jnp.sum(z * half_way, axis=1, keepdims=True) / scale[:, :1]
            trans = jnp.sqrt((members - 1.0) / scale) * z + mean_weight
            trans_out[first + b] = trans.astype(jnp.bfloat16)

    spread_lists(0)
    for k in order:
        peer = z_peers[k]
        from_z(peer).wait_recv()
        for side in range(2):
            near(side, peer, pert_all.at[1, peer]).start()
    add_piece(1)
    for side in range(2):
        info(side).wait()
        for i in range(nm):
            near(side, i, pert_all.at[1, i]).wait()
        add_piece(2 * side)
    for peer in z_peers:
        to_z(peer).wait_send()
    roots_and_weights(0)
    if ns > group:

        def more(g, carry):
            spread_lists(g * group)
            for piece in range(3):
                add_piece(piece)
            roots_and_weights(g * group)
            return carry

        lax.fori_loop(1, ns // group, more, 0)

    def to_tile(peer):
        return remote(trans_out.at[peer], trans_in.at[s], t_send.at[peer], t_recv.at[s], (peer, m))

    def from_tile(peer):
        return remote(trans_out.at[peer], trans_in.at[peer], t_send.at[peer], t_recv.at[peer], (peer, m))

    for peer in s_peers:
        to_tile(peer).start()
    trans_in[s] = trans_out[s]
    for peer in s_peers:
        from_tile(peer).wait_recv()

    def mix(o, carry):
        total = jnp.zeros((members, LANES), jnp.float32)
        for i in range(ns):
            total += coef_ref[o, m * ns + i] * trans_in[i].astype(jnp.float32)
        mixed[o] = total
        return carry

    def up(o):
        return remote(
            up_out.at[o], up_in.at[o], up_send.at[o], up_recv.at[o], (s, lax.rem(m + 1, nm))
        )

    def down(o):
        return remote(
            down_out.at[o], down_in.at[o], down_send.at[o], down_recv.at[o],
            (s, lax.rem(m + nm - 1, nm)),
        )

    def first_hop(o, carry):
        mix(o, carry)

        @pl.when(m == 0)
        def _():
            up_out[o] = mixed[o].astype(jnp.bfloat16)
            up(o).start()

        @pl.when(m == nm - 1)
        def _():
            down_out[o] = mixed[o].astype(jnp.bfloat16)
            down(o).start()

        return carry

    lax.fori_loop(0, oblocks, first_hop, 0)

    def later_hops(o, carry):
        @pl.when(m > 0)
        def _():
            up(o).wait_recv()

        @pl.when(jnp.logical_and(m > 0, m < nm - 1))
        def _():
            up_out[o] = (mixed[o] + up_in[o].astype(jnp.float32)).astype(jnp.bfloat16)
            up(o).start()

        @pl.when(m < nm - 1)
        def _():
            down(o).wait_recv()

        @pl.when(jnp.logical_and(m > 0, m < nm - 1))
        def _():
            down_out[o] = (mixed[o] + down_in[o].astype(jnp.float32)).astype(jnp.bfloat16)
            down(o).start()

        @pl.when(m == 0)
        def _():
            out_ref[o] = (mixed[o] + down_in[o].astype(jnp.float32)).astype(jnp.bfloat16)

        @pl.when(m == nm - 1)
        def _():
            out_ref[o] = (mixed[o] + up_in[o].astype(jnp.float32)).astype(jnp.bfloat16)

        @pl.when(jnp.logical_and(m > 0, m < nm - 1))
        def _():
            both = up_in[o].astype(jnp.float32) + down_in[o].astype(jnp.float32)
            out_ref[o] = (mixed[o] + both).astype(jnp.bfloat16)

        return carry

    lax.fori_loop(0, oblocks, later_hops, 0)

    def drain(o, carry):
        @pl.when(m < nm - 1)
        def _():
            up(o).wait_send()

        @pl.when(m > 0)
        def _():
            down(o).wait_send()

        return carry

    lax.fori_loop(0, oblocks, drain, 0)
    for peer in s_peers:
        to_tile(peer).wait_send()


def mixed_weights(send, coef, lists, loc, pert, extra):
    ns, nm = lax.axis_size("space"), lax.axis_size("member")
    shard, tile_obs = pert.shape
    members = shard * nm
    group = 8 if ns % 8 == 0 else ns
    oblocks = coef.shape[0]
    his = 3 * tile_obs // LANES
    vmem = pl.BlockSpec(memory_space=pltpu.VMEM)
    smem = pl.BlockSpec(memory_space=pltpu.SMEM)
    dma = pltpu.SemaphoreType.DMA
    blocks = lambda n, kind: pltpu.VMEM((n, members, LANES), kind)
    return pl.pallas_call(
        functools.partial(letkf_kernel, group, ns, nm),
        in_specs=[smem, smem, vmem, vmem, vmem, vmem],
        out_specs=vmem,
        out_shape=jax.ShapeDtypeStruct((oblocks, members, LANES), jnp.bfloat16),
        scratch_shapes=[
            pltpu.VMEM((3, nm, shard, tile_obs), jnp.bfloat16),
            pltpu.VMEM((3,) + extra.shape, jnp.bfloat16),
            pltpu.VMEM(loc.shape, jnp.float32),
            pltpu.VMEM((group, his, LANES), jnp.float32),
            blocks(group, jnp.float32),
            blocks(group, jnp.float32),
            blocks(group, jnp.float32),
            pltpu.VMEM((group, members, 1), jnp.float32),
            pltpu.VMEM((group, 1, LANES), jnp.float32),
            blocks(ns, jnp.bfloat16),
            blocks(ns, jnp.bfloat16),
            blocks(oblocks, jnp.bfloat16),
            blocks(oblocks, jnp.bfloat16),
            blocks(oblocks, jnp.bfloat16),
            blocks(oblocks, jnp.bfloat16),
            blocks(oblocks, jnp.float32),
            dma((nm,)), dma((nm,)), dma((2, nm)), dma((2, nm)), dma((2,)), dma((2,)),
            dma((ns,)), dma((ns,)),
            dma((oblocks,)), dma((oblocks,)), dma((oblocks,)), dma((oblocks,)),
        ],
        compiler_params=pltpu.CompilerParams(collective_id=0, has_side_effects=True),
        name="mixed_weights",
    )(send, coef, lists, loc, pert, extra)


def apply_weights(ensemble, mixed):
    ens_mean = jnp.mean(ensemble, axis=0, dtype=jnp.float32)
    deviation = (ensemble.astype(jnp.float32) - ens_mean[None]).astype(jnp.bfloat16)
    product = jnp.einsum("jol,oji->iol", deviation, mixed, preferred_element_type=jnp.float32)
    return (ens_mean[None] + product).astype(jnp.bfloat16)


def shards(
    obs_pert,
    innovation,
    obs_prec,
    obs_lists,
    loc_weight,
    send_rows,
    ocean_src,
    ocean_frac,
    ocean_ens,
):
    tile_obs = obs_pert.shape[1]
    extra = jnp.zeros((16, tile_obs), jnp.bfloat16).at[0].set(innovation).at[1].set(obs_prec)
    slots = jnp.arange(lax.axis_size("space") * lax.axis_size("member"), dtype=jnp.int32)[None]
    frac = ocean_frac[:, None]
    coef = jnp.where(ocean_src[:, :1] == slots, 1.0 - frac, 0.0) + jnp.where(
        ocean_src[:, 1:] == slots, frac, 0.0
    )
    mixed = mixed_weights(send_rows[0], coef, obs_lists, loc_weight, obs_pert, extra)
    mixed = mixed[:, :, : ocean_ens.shape[0]]
    return apply_weights(ocean_ens, mixed)


def solution(mesh):
    return jax.shard_map(
        shards,
        mesh=mesh,
        in_specs=(
            P("member", "space"),
            P("space"),
            P("space"),
            P("space", None),
            P("space", None),
            P("space", None, None),
            P("space", None),
            P("space"),
            P(None, "space", "member"),
        ),
        out_specs=P(None, "space", "member"),
        check_vma=False,
    )
```

```python
import functools

import jax
import jax.numpy as jnp
from jax import lax
from jax.experimental import pallas as pl
from jax.experimental.pallas import tpu as pltpu
from jax.sharding import PartitionSpec as P

ITERS = 12
LANES = 128
CHUNK = 512


def split(value):
    high = value.astype(jnp.bfloat16)
    low = (value - high.astype(jnp.float32)).astype(jnp.bfloat16)
    return high, low


def left_side(value):
    return jnp.concatenate(split(value), axis=1)


def right_side(value):
    pair = left_side(value)
    filler = jnp.zeros((LANES - pair.shape[0], pair.shape[1]), jnp.bfloat16)
    return jnp.concatenate([pair, filler, pair, filler], axis=0)


def halves(product):
    return product[:, :LANES] + product[:, LANES:]


def mm(lhs, rhs):
    return jnp.dot(lhs, rhs, preferred_element_type=jnp.float32)


MESH = pl.DeviceIdType.MESH


def remote(src, dst, send_sem, recv_sem, device):
    return pltpu.make_async_remote_copy(
        src_ref=src, dst_ref=dst, send_sem=send_sem, recv_sem=recv_sem,
        device_id=device, device_id_type=MESH,
    )


def letkf_kernel(
    group, ns, nm,
    send_ref, coef_ref, lists_hbm, loc_hbm, pert_ref, extra_ref, out_ref,
    lists_ref, loc_ref, local_sem, pert_all, extra_all, loc_f32, dense, gram, root, inverse, pulled, scales,
    trans_out, trans_in, up_out, up_in, down_out, down_in, mixed,
    z_send, z_recv, near_send, near_recv, info_send, info_recv, t_send, t_recv,
    up_send, up_recv, down_send, down_recv,
):
    s = lax.axis_index("space")
    m = lax.axis_index("member")
    members = pert_ref.shape[0] * nm
    tile_obs = pert_ref.shape[1]
    tile_his = tile_obs // LANES
    group_len = lists_ref.shape[0] // nm
    take_lists = pltpu.make_async_copy(lists_hbm, lists_ref, local_sem.at[0])
    take_loc = pltpu.make_async_copy(loc_hbm, loc_ref, local_sem.at[1])
    take_pert = pltpu.make_async_copy(pert_ref, pert_all.at[1, m], local_sem.at[2])
    for copy in (take_lists, take_loc, take_pert):
        copy.start()
    oblocks = out_ref.shape[0]
    z_peers = [lax.rem(m + k, nm) for k in range(1, nm)]
    s_peers = [lax.rem(s + k, ns) for k in range(1, ns)]
    left, right = lax.rem(s + ns - 1, ns), lax.rem(s + 1, ns)

    barrier = pltpu.get_barrier_semaphore()
    for peer in z_peers:
        pl.semaphore_signal(barrier, inc=1, device_id=(s, peer), device_id_type=MESH)
    for peer in s_peers:
        pl.semaphore_signal(barrier, inc=1, device_id=(peer, m), device_id_type=MESH)
    pl.semaphore_wait(barrier, len(z_peers) + len(s_peers))

    def to_z(peer):
        return remote(pert_ref, pert_all.at[1, m], z_send.at[peer], z_recv.at[m], (s, peer))

    def from_z(peer):
        return remote(pert_ref, pert_all.at[1, peer], z_send.at[m], z_recv.at[peer], (s, peer))

    def near(side, owner, src):
        target = right if side == 0 else left
        return remote(
            src, pert_all.at[2 * side, owner], near_send.at[side, owner],
            near_recv.at[side, owner], (target, m),
        )

    def info(side):
        target = right if side == 0 else left
        return remote(
            extra_ref, extra_all.at[2 * side], info_send.at[side], info_recv.at[side], (target, m)
        )

    order = sorted(range(nm - 1), key=lambda k: abs(k + 1 - nm / 2))
    for k in order:
        to_z(z_peers[k]).start()
    for side in range(2):
        near(side, m, pert_ref).start()
        info(side).start()
    extra_all[1] = extra_ref[...]
    take_lists.wait()
    take_loc.wait()
    take_pert.wait()
    loc_f32[...] = loc_ref[...].astype(jnp.float32)

    his = dense.shape[1]
    lobs = lists_ref.shape[1]
    hi_iota = lax.broadcasted_iota(jnp.int32, (his, lobs), 0)
    lo_iota = lax.broadcasted_iota(jnp.int32, (LANES, lobs), 0)
    rows = lax.broadcasted_iota(jnp.int32, (members, LANES), 0)
    cols = lax.broadcasted_iota(jnp.int32, (members, LANES), 1)
    on_diag = rows == cols
    half3 = jnp.where(on_diag, 1.5, 0.0)
    per = CHUNK // LANES

    def spread_lists(first):
        for b in range(group):
            row = send_ref[m, first + b] + m * group_len
            spots = lists_ref[pl.ds(row, 1), :]
            taper = loc_f32[pl.ds(row, 1), :]
            high, low = lax.shift_right_logical(spots, 7), jnp.bitwise_and(spots, LANES - 1)
            hi_hot = jnp.where(hi_iota == high, taper, 0.0).astype(jnp.bfloat16)
            lo_hot = jnp.where(lo_iota == low, 1.0, 0.0).astype(jnp.bfloat16)
            dense[b] = lax.dot_general(
                hi_hot, lo_hot, (((1,), (1,)), ((), ())), preferred_element_type=jnp.float32
            )
        gram[...] = jnp.zeros_like(gram)

    def add_piece(piece):
        def chunk_step(c, carry):
            span = pl.ds(pl.multiple_of(c * CHUNK, CHUNK), CHUNK)
            wide = jnp.concatenate(
                [pert_all[piece, i, :, span].astype(jnp.float32) for i in range(nm)], axis=0
            )
            extra = extra_all[piece, :, span]
            cells = jnp.concatenate([wide.astype(jnp.bfloat16), extra], axis=0)
            wide = wide * extra.astype(jnp.float32)[1:2]
            contract = (((1,), (1,)), ((), ()))
            for b in range(group):
                parts = []
                for j in range(per):
                    weight = dense[b, pl.ds(piece * tile_his + c * per + j, 1), :]
                    parts.append(wide[:, j * LANES : (j + 1) * LANES] * weight)
                high, low = split(jnp.concatenate(parts, axis=1))
                gram[b, :, : cells.shape[0]] += lax.dot_general(
                    high, cells, contract, preferred_element_type=jnp.float32
                ) + lax.dot_general(low, cells, contract, preferred_element_type=jnp.float32)
            return carry

        lax.fori_loop(0, tile_obs // CHUNK, chunk_step, 0)

    def roots_and_weights(first):
        for b in range(group):
            both = gram[b]
            pulled[b] = jnp.sum(jnp.where(cols == members, both, 0.0), axis=1, keepdims=True)
            matrix = jnp.where(cols < members, both, 0.0) + jnp.where(on_diag, members - 1.0, 0.0)
            scale = jnp.sum(
                jnp.sum(jnp.where(on_diag, matrix, 0.0), axis=1, keepdims=True),
                axis=0, keepdims=True,
            )
            scales[b] = jnp.broadcast_to(scale, (1, LANES))
            start = matrix / scale
            correction = half3 - 0.5 * start
            root[b] = halves(mm(left_side(start), right_side(correction)))
            inverse[b] = correction

        def newton(step, carry):
            corrections, pairs = [], []
            filler = jnp.zeros((LANES - members, 2 * LANES), jnp.bfloat16)
            for b in range(group):
                r, z = left_side(root[b]), left_side(inverse[b])
                rhs = jnp.concatenate([r, filler, r, filler], axis=0)
                corrections.append(half3 - 0.5 * halves(mm(z, rhs)))
                pairs.append(jnp.concatenate([r, z], axis=0))
            for b in range(group):
                both = halves(mm(pairs[b], right_side(corrections[b])))
                root[b] = both[:members]
                inverse[b] = both[members:]
            return carry

        lax.fori_loop(0, ITERS - 1, newton, 0)
        for b in range(group):
            z = inverse[b]
            scale = scales[b]
            half_way = jnp.sum(z * pulled[b], axis=0, keepdims=True)
            mean_weight = jnp.sum(z * half_way, axis=1, keepdims=True) / scale[:, :1]
            trans = jnp.sqrt((members - 1.0) / scale) * z + mean_weight
            trans_out[first + b] = trans.astype(jnp.bfloat16)

    spread_lists(0)
    for k in order:
        peer = z_peers[k]
        from_z(peer).wait_recv()
        for side in range(2):
            near(side, peer, pert_all.at[1, peer]).start()
    add_piece(1)
    for side in range(2):
        info(side).wait()
        for i in range(nm):
            near(side, i, pert_all.at[1, i]).wait()
        add_piece(2 * side)
    for peer in z_peers:
        to_z(peer).wait_send()
    roots_and_weights(0)
    if ns > group:

        def more(g, carry):
            spread_lists(g * group)
            for piece in range(3):
                add_piece(piece)
            roots_and_weights(g * group)
            return carry

        lax.fori_loop(1, ns // group, more, 0)

    def to_tile(peer):
        return remote(trans_out.at[peer], trans_in.at[s], t_send.at[peer], t_recv.at[s], (peer, m))

    def from_tile(peer):
        return remote(trans_out.at[peer], trans_in.at[peer], t_send.at[peer], t_recv.at[peer], (peer, m))

    for peer in s_peers:
        to_tile(peer).start()
    trans_in[s] = trans_out[s]
    for peer in s_peers:
        from_tile(peer).wait_recv()

    def mix(o, carry):
        total = jnp.zeros((members, LANES), jnp.float32)
        for i in range(ns):
            total += coef_ref[o, m * ns + i] * trans_in[i].astype(jnp.float32)
        mixed[o] = total
        return carry

    def up(o):
        return remote(
            up_out.at[o], up_in.at[o], up_send.at[o], up_recv.at[o], (s, lax.rem(m + 1, nm))
        )

    def down(o):
        return remote(
            down_out.at[o], down_in.at[o], down_send.at[o], down_recv.at[o],
            (s, lax.rem(m + nm - 1, nm)),
        )

    def first_hop(o, carry):
        mix(o, carry)

        @pl.when(m == 0)
        def _():
            up_out[o] = mixed[o].astype(jnp.bfloat16)
            up(o).start()

        @pl.when(m == nm - 1)
        def _():
            down_out[o] = mixed[o].astype(jnp.bfloat16)
            down(o).start()

        return carry

    lax.fori_loop(0, oblocks, first_hop, 0)

    def pass_up(o, carry):
        up(o).wait_recv()

        @pl.when(m < nm - 1)
        def _():
            up_out[o] = (mixed[o] + up_in[o].astype(jnp.float32)).astype(jnp.bfloat16)
            up(o).start()

        return carry

    def pass_down(o, carry):
        down(o).wait_recv()

        @pl.when(m > 0)
        def _():
            down_out[o] = (mixed[o] + down_in[o].astype(jnp.float32)).astype(jnp.bfloat16)
            down(o).start()

        return carry

    lower = m < nm // 2

    @pl.when(jnp.logical_and(lower, m > 0))
    def _():
        lax.fori_loop(0, oblocks, pass_up, 0)

    @pl.when(m < nm - 1)
    def _():
        lax.fori_loop(0, oblocks, pass_down, 0)

    @pl.when(jnp.logical_not(lower))
    def _():
        lax.fori_loop(0, oblocks, pass_up, 0)

    def finish(o, carry):
        @pl.when(m == 0)
        def _():
            out_ref[o] = (mixed[o] + down_in[o].astype(jnp.float32)).astype(jnp.bfloat16)

        @pl.when(m == nm - 1)
        def _():
            out_ref[o] = (mixed[o] + up_in[o].astype(jnp.float32)).astype(jnp.bfloat16)

        @pl.when(jnp.logical_and(m > 0, m < nm - 1))
        def _():
            both = up_in[o].astype(jnp.float32) + down_in[o].astype(jnp.float32)
            out_ref[o] = (mixed[o] + both).astype(jnp.bfloat16)

        return carry

    lax.fori_loop(0, oblocks, finish, 0)

    def drain(o, carry):
        @pl.when(m < nm - 1)
        def _():
            up(o).wait_send()

        @pl.when(m > 0)
        def _():
            down(o).wait_send()

        return carry

    lax.fori_loop(0, oblocks, drain, 0)
    for peer in s_peers:
        to_tile(peer).wait_send()


def mixed_weights(send, coef, lists, loc, pert, extra):
    ns, nm = lax.axis_size("space"), lax.axis_size("member")
    shard, tile_obs = pert.shape
    members = shard * nm
    group = 8 if ns % 8 == 0 else ns
    oblocks = coef.shape[0]
    his = 3 * tile_obs // LANES
    vmem = pl.BlockSpec(memory_space=pltpu.VMEM)
    hbm = pl.BlockSpec(memory_space=pl.ANY)
    smem = pl.BlockSpec(memory_space=pltpu.SMEM)
    dma = pltpu.SemaphoreType.DMA
    blocks = lambda n, kind: pltpu.VMEM((n, members, LANES), kind)
    return pl.pallas_call(
        functools.partial(letkf_kernel, group, ns, nm),
        in_specs=[smem, smem, hbm, hbm, hbm, vmem],
        out_specs=vmem,
        out_shape=jax.ShapeDtypeStruct((oblocks, members, LANES), jnp.bfloat16),
        scratch_shapes=[
            pltpu.VMEM(lists.shape, lists.dtype),
            pltpu.VMEM(loc.shape, loc.dtype),
            dma((3,)),
            pltpu.VMEM((3, nm, shard, tile_obs), jnp.bfloat16),
            pltpu.VMEM((3,) + extra.shape, jnp.bfloat16),
            pltpu.VMEM(loc.shape, jnp.float32),
            pltpu.VMEM((group, his, LANES), jnp.float32),
            blocks(group, jnp.float32),
            blocks(group, jnp.float32),
            blocks(group, jnp.float32),
            pltpu.VMEM((group, members, 1), jnp.float32),
            pltpu.VMEM((group, 1, LANES), jnp.float32),
            blocks(ns, jnp.bfloat16),
            blocks(ns, jnp.bfloat16),
            blocks(oblocks, jnp.bfloat16),
            blocks(oblocks, jnp.bfloat16),
            blocks(oblocks, jnp.bfloat16),
            blocks(oblocks, jnp.bfloat16),
            blocks(oblocks, jnp.float32),
            dma((nm,)), dma((nm,)), dma((2, nm)), dma((2, nm)), dma((2,)), dma((2,)),
            dma((ns,)), dma((ns,)),
            dma((oblocks,)), dma((oblocks,)), dma((oblocks,)), dma((oblocks,)),
        ],
        compiler_params=pltpu.CompilerParams(collective_id=0, has_side_effects=True),
        name="mixed_weights",
    )(send, coef, lists, loc, pert, extra)


def apply_weights(ensemble, mixed):
    ens_mean = jnp.mean(ensemble, axis=0, dtype=jnp.float32)
    deviation = (ensemble.astype(jnp.float32) - ens_mean[None]).astype(jnp.bfloat16)
    product = jnp.einsum("jol,oji->iol", deviation, mixed, preferred_element_type=jnp.float32)
    return (ens_mean[None] + product).astype(jnp.bfloat16)


def shards(
    obs_pert,
    innovation,
    obs_prec,
    obs_lists,
    loc_weight,
    send_rows,
    ocean_src,
    ocean_frac,
    ocean_ens,
):
    tile_obs = obs_pert.shape[1]
    extra = jnp.zeros((16, tile_obs), jnp.bfloat16).at[0].set(innovation).at[1].set(obs_prec)
    slots = jnp.arange(lax.axis_size("space") * lax.axis_size("member"), dtype=jnp.int32)[None]
    frac = ocean_frac[:, None]
    coef = jnp.where(ocean_src[:, :1] == slots, 1.0 - frac, 0.0) + jnp.where(
        ocean_src[:, 1:] == slots, frac, 0.0
    )
    mixed = mixed_weights(send_rows[0], coef, obs_lists, loc_weight, obs_pert, extra)
    mixed = mixed[:, :, : ocean_ens.shape[0]]
    return apply_weights(ocean_ens, mixed)


def solution(mesh):
    return jax.shard_map(
        shards,
        mesh=mesh,
        in_specs=(
            P("member", "space"),
            P("space"),
            P("space"),
            P("space", None),
            P("space", None),
            P("space", None, None),
            P("space", None),
            P("space"),
            P(None, "space", "member"),
        ),
        out_specs=P(None, "space", "member"),
        check_vma=False,
    )
```

```python
import functools

import jax
import jax.numpy as jnp
from jax import lax
from jax.experimental import pallas as pl
from jax.experimental.pallas import tpu as pltpu
from jax.sharding import PartitionSpec as P

ITERS = 12
LANES = 128
CHUNK = 512


def split(value):
    high = value.astype(jnp.bfloat16)
    low = (value - high.astype(jnp.float32)).astype(jnp.bfloat16)
    return high, low


def left_side(value):
    return jnp.concatenate(split(value), axis=1)


def right_side(value):
    pair = left_side(value)
    filler = jnp.zeros((LANES - pair.shape[0], pair.shape[1]), jnp.bfloat16)
    return jnp.concatenate([pair, filler, pair, filler], axis=0)


def halves(product):
    return product[:, :LANES] + product[:, LANES:]


def mm(lhs, rhs):
    return jnp.dot(lhs, rhs, preferred_element_type=jnp.float32)


MESH = pl.DeviceIdType.MESH


def remote(src, dst, send_sem, recv_sem, device):
    return pltpu.make_async_remote_copy(
        src_ref=src, dst_ref=dst, send_sem=send_sem, recv_sem=recv_sem,
        device_id=device, device_id_type=MESH,
    )


def letkf_kernel(
    group, ns, nm,
    send_ref, src_ref, frac_ref, lists_hbm, loc_hbm, pert_ref, extra_ref, out_ref,
    lists_ref, loc_ref, local_sem, pert_all, extra_all, loc_f32, dense, gram, root, inverse, pulled, scales,
    trans_out, trans_in, up_out, up_in, down_out, down_in, mixed,
    z_send, z_recv, near_send, near_recv, info_send, info_recv, t_send, t_recv,
    up_send, up_recv, down_send, down_recv,
):
    s = lax.axis_index("space")
    m = lax.axis_index("member")
    members = pert_ref.shape[0] * nm
    tile_obs = pert_ref.shape[1]
    tile_his = tile_obs // LANES
    group_len = lists_ref.shape[0] // nm
    take_lists = pltpu.make_async_copy(lists_hbm, lists_ref, local_sem.at[0])
    take_loc = pltpu.make_async_copy(loc_hbm, loc_ref, local_sem.at[1])
    take_pert = pltpu.make_async_copy(pert_ref, pert_all.at[1, m], local_sem.at[2])
    for copy in (take_lists, take_loc, take_pert):
        copy.start()
    oblocks = out_ref.shape[0]
    z_peers = [lax.rem(m + k, nm) for k in range(1, nm)]
    s_peers = [lax.rem(s + k, ns) for k in range(1, ns)]
    left, right = lax.rem(s + ns - 1, ns), lax.rem(s + 1, ns)

    barrier = pltpu.get_barrier_semaphore()
    for peer in z_peers:
        pl.semaphore_signal(barrier, inc=1, device_id=(s, peer), device_id_type=MESH)
    for peer in s_peers:
        pl.semaphore_signal(barrier, inc=1, device_id=(peer, m), device_id_type=MESH)
    pl.semaphore_wait(barrier, len(z_peers) + len(s_peers))

    def to_z(peer):
        return remote(pert_ref, pert_all.at[1, m], z_send.at[peer], z_recv.at[m], (s, peer))

    def from_z(peer):
        return remote(pert_ref, pert_all.at[1, peer], z_send.at[m], z_recv.at[peer], (s, peer))

    def near(side, owner, src):
        target = right if side == 0 else left
        return remote(
            src, pert_all.at[2 * side, owner], near_send.at[side, owner],
            near_recv.at[side, owner], (target, m),
        )

    def info(side):
        target = right if side == 0 else left
        return remote(
            extra_ref, extra_all.at[2 * side], info_send.at[side], info_recv.at[side], (target, m)
        )

    order = sorted(range(nm - 1), key=lambda k: abs(k + 1 - nm / 2))
    for k in order:
        to_z(z_peers[k]).start()
    for side in range(2):
        near(side, m, pert_ref).start()
        info(side).start()
    extra_all[1] = extra_ref[...]
    take_lists.wait()
    take_loc.wait()
    take_pert.wait()
    loc_f32[...] = loc_ref[...].astype(jnp.float32)

    his = dense.shape[1]
    lobs = lists_ref.shape[1]
    hi_iota = lax.broadcasted_iota(jnp.int32, (his, lobs), 0)
    lo_iota = lax.broadcasted_iota(jnp.int32, (LANES, lobs), 0)
    rows = lax.broadcasted_iota(jnp.int32, (members, LANES), 0)
    cols = lax.broadcasted_iota(jnp.int32, (members, LANES), 1)
    on_diag = rows == cols
    half3 = jnp.where(on_diag, 1.5, 0.0)
    per = CHUNK // LANES

    def spread_lists(first):
        for b in range(group):
            row = send_ref[m, first + b] + m * group_len
            spots = lists_ref[pl.ds(row, 1), :]
            taper = loc_f32[pl.ds(row, 1), :]
            high, low = lax.shift_right_logical(spots, 7), jnp.bitwise_and(spots, LANES - 1)
            hi_hot = jnp.where(hi_iota == high, taper, 0.0).astype(jnp.bfloat16)
            lo_hot = jnp.where(lo_iota == low, 1.0, 0.0).astype(jnp.bfloat16)
            dense[b] = lax.dot_general(
                hi_hot, lo_hot, (((1,), (1,)), ((), ())), preferred_element_type=jnp.float32
            )
        gram[...] = jnp.zeros_like(gram)

    def add_piece(piece):
        def chunk_step(c, carry):
            span = pl.ds(pl.multiple_of(c * CHUNK, CHUNK), CHUNK)
            wide = jnp.concatenate(
                [pert_all[piece, i, :, span].astype(jnp.float32) for i in range(nm)], axis=0
            )
            extra = extra_all[piece, :, span]
            cells = jnp.concatenate([wide.astype(jnp.bfloat16), extra], axis=0)
            wide = wide * extra.astype(jnp.float32)[1:2]
            contract = (((1,), (1,)), ((), ()))
            for b in range(group):
                parts = []
                for j in range(per):
                    weight = dense[b, pl.ds(piece * tile_his + c * per + j, 1), :]
                    parts.append(wide[:, j * LANES : (j + 1) * LANES] * weight)
                high, low = split(jnp.concatenate(parts, axis=1))
                gram[b, :, : cells.shape[0]] += lax.dot_general(
                    high, cells, contract, preferred_element_type=jnp.float32
                ) + lax.dot_general(low, cells, contract, preferred_element_type=jnp.float32)
            return carry

        lax.fori_loop(0, tile_obs // CHUNK, chunk_step, 0)

    def roots_and_weights(first):
        for b in range(group):
            both = gram[b]
            pulled[b] = jnp.sum(jnp.where(cols == members, both, 0.0), axis=1, keepdims=True)
            matrix = jnp.where(cols < members, both, 0.0) + jnp.where(on_diag, members - 1.0, 0.0)
            scale = jnp.sum(
                jnp.sum(jnp.where(on_diag, matrix, 0.0), axis=1, keepdims=True),
                axis=0, keepdims=True,
            )
            scales[b] = jnp.broadcast_to(scale, (1, LANES))
            start = matrix / scale
            correction = half3 - 0.5 * start
            root[b] = halves(mm(left_side(start), right_side(correction)))
            inverse[b] = correction

        def newton(step, carry):
            corrections, pairs = [], []
            filler = jnp.zeros((LANES - members, 2 * LANES), jnp.bfloat16)
            for b in range(group):
                r, z = left_side(root[b]), left_side(inverse[b])
                rhs = jnp.concatenate([r, filler, r, filler], axis=0)
                corrections.append(half3 - 0.5 * halves(mm(z, rhs)))
                pairs.append(jnp.concatenate([r, z], axis=0))
            for b in range(group):
                both = halves(mm(pairs[b], right_side(corrections[b])))
                root[b] = both[:members]
                inverse[b] = both[members:]
            return carry

        lax.fori_loop(0, ITERS - 1, newton, 0)
        for b in range(group):
            z = inverse[b]
            scale = scales[b]
            half_way = jnp.sum(z * pulled[b], axis=0, keepdims=True)
            mean_weight = jnp.sum(z * half_way, axis=1, keepdims=True) / scale[:, :1]
            trans = jnp.sqrt((members - 1.0) / scale) * z + mean_weight
            trans_out[first + b] = trans.astype(jnp.bfloat16)

    spread_lists(0)
    for k in order:
        peer = z_peers[k]
        from_z(peer).wait_recv()
        for side in range(2):
            near(side, peer, pert_all.at[1, peer]).start()
    add_piece(1)
    for side in range(2):
        info(side).wait()
        for i in range(nm):
            near(side, i, pert_all.at[1, i]).wait()
        add_piece(2 * side)
    for peer in z_peers:
        to_z(peer).wait_send()
    roots_and_weights(0)
    if ns > group:

        def more(g, carry):
            spread_lists(g * group)
            for piece in range(3):
                add_piece(piece)
            roots_and_weights(g * group)
            return carry

        lax.fori_loop(1, ns // group, more, 0)

    def to_tile(peer):
        return remote(trans_out.at[peer], trans_in.at[s], t_send.at[peer], t_recv.at[s], (peer, m))

    def from_tile(peer):
        return remote(trans_out.at[peer], trans_in.at[peer], t_send.at[peer], t_recv.at[peer], (peer, m))

    for peer in s_peers:
        to_tile(peer).start()
    trans_in[s] = trans_out[s]
    for peer in s_peers:
        from_tile(peer).wait_recv()

    def mix(o, carry):
        total = jnp.zeros((members, LANES), jnp.float32)
        one, two, frac = src_ref[o, 0], src_ref[o, 1], frac_ref[o]
        for i in range(ns):
            slot = m * ns + i
            weight = jnp.where(one == slot, 1.0 - frac, 0.0) + jnp.where(two == slot, frac, 0.0)
            total += weight * trans_in[i].astype(jnp.float32)
        mixed[o] = total
        return carry

    def up(o):
        return remote(
            up_out.at[o], up_in.at[o], up_send.at[o], up_recv.at[o], (s, lax.rem(m + 1, nm))
        )

    def down(o):
        return remote(
            down_out.at[o], down_in.at[o], down_send.at[o], down_recv.at[o],
            (s, lax.rem(m + nm - 1, nm)),
        )

    def first_hop(o, carry):
        mix(o, carry)

        @pl.when(m == 0)
        def _():
            up_out[o] = mixed[o].astype(jnp.bfloat16)
            up(o).start()

        @pl.when(m == nm - 1)
        def _():
            down_out[o] = mixed[o].astype(jnp.bfloat16)
            down(o).start()

        return carry

    lax.fori_loop(0, oblocks, first_hop, 0)

    def pass_up(o, carry):
        up(o).wait_recv()

        @pl.when(m < nm - 1)
        def _():
            up_out[o] = (mixed[o] + up_in[o].astype(jnp.float32)).astype(jnp.bfloat16)
            up(o).start()

        return carry

    def pass_down(o, carry):
        down(o).wait_recv()

        @pl.when(m > 0)
        def _():
            down_out[o] = (mixed[o] + down_in[o].astype(jnp.float32)).astype(jnp.bfloat16)
            down(o).start()

        return carry

    lower = m < nm // 2

    @pl.when(jnp.logical_and(lower, m > 0))
    def _():
        lax.fori_loop(0, oblocks, pass_up, 0)

    @pl.when(m < nm - 1)
    def _():
        lax.fori_loop(0, oblocks, pass_down, 0)

    @pl.when(jnp.logical_not(lower))
    def _():
        lax.fori_loop(0, oblocks, pass_up, 0)

    def finish(o, carry):
        @pl.when(m == 0)
        def _():
            out_ref[o] = (mixed[o] + down_in[o].astype(jnp.float32)).astype(jnp.bfloat16)

        @pl.when(m == nm - 1)
        def _():
            out_ref[o] = (mixed[o] + up_in[o].astype(jnp.float32)).astype(jnp.bfloat16)

        @pl.when(jnp.logical_and(m > 0, m < nm - 1))
        def _():
            both = up_in[o].astype(jnp.float32) + down_in[o].astype(jnp.float32)
            out_ref[o] = (mixed[o] + both).astype(jnp.bfloat16)

        return carry

    lax.fori_loop(0, oblocks, finish, 0)

    def drain(o, carry):
        @pl.when(m < nm - 1)
        def _():
            up(o).wait_send()

        @pl.when(m > 0)
        def _():
            down(o).wait_send()

        return carry

    lax.fori_loop(0, oblocks, drain, 0)
    for peer in s_peers:
        to_tile(peer).wait_send()


def mixed_weights(send, src, frac, lists, loc, pert, extra):
    ns, nm = lax.axis_size("space"), lax.axis_size("member")
    shard, tile_obs = pert.shape
    members = shard * nm
    group = 8 if ns % 8 == 0 else ns
    oblocks = src.shape[0]
    his = 3 * tile_obs // LANES
    vmem = pl.BlockSpec(memory_space=pltpu.VMEM)
    hbm = pl.BlockSpec(memory_space=pl.ANY)
    smem = pl.BlockSpec(memory_space=pltpu.SMEM)
    dma = pltpu.SemaphoreType.DMA
    blocks = lambda n, kind: pltpu.VMEM((n, members, LANES), kind)
    return pl.pallas_call(
        functools.partial(letkf_kernel, group, ns, nm),
        in_specs=[smem, smem, smem, hbm, hbm, hbm, vmem],
        out_specs=vmem,
        out_shape=jax.ShapeDtypeStruct((oblocks, members, LANES), jnp.bfloat16),
        scratch_shapes=[
            pltpu.VMEM(lists.shape, lists.dtype),
            pltpu.VMEM(loc.shape, loc.dtype),
            dma((3,)),
            pltpu.VMEM((3, nm, shard, tile_obs), jnp.bfloat16),
            pltpu.VMEM((3,) + extra.shape, jnp.bfloat16),
            pltpu.VMEM(loc.shape, jnp.float32),
            pltpu.VMEM((group, his, LANES), jnp.float32),
            blocks(group, jnp.float32),
            blocks(group, jnp.float32),
            blocks(group, jnp.float32),
            pltpu.VMEM((group, members, 1), jnp.float32),
            pltpu.VMEM((group, 1, LANES), jnp.float32),
            blocks(ns, jnp.bfloat16),
            blocks(ns, jnp.bfloat16),
            blocks(oblocks, jnp.bfloat16),
            blocks(oblocks, jnp.bfloat16),
            blocks(oblocks, jnp.bfloat16),
            blocks(oblocks, jnp.bfloat16),
            blocks(oblocks, jnp.float32),
            dma((nm,)), dma((nm,)), dma((2, nm)), dma((2, nm)), dma((2,)), dma((2,)),
            dma((ns,)), dma((ns,)),
            dma((oblocks,)), dma((oblocks,)), dma((oblocks,)), dma((oblocks,)),
        ],
        compiler_params=pltpu.CompilerParams(collective_id=0, has_side_effects=True),
        name="mixed_weights",
    )(send, src, frac, lists, loc, pert, extra)


def apply_weights(ensemble, mixed):
    ens_mean = jnp.mean(ensemble, axis=0, dtype=jnp.float32)
    deviation = (ensemble.astype(jnp.float32) - ens_mean[None]).astype(jnp.bfloat16)
    product = jnp.einsum("jol,oji->iol", deviation, mixed, preferred_element_type=jnp.float32)
    return (ens_mean[None] + product).astype(jnp.bfloat16)


def shards(
    obs_pert,
    innovation,
    obs_prec,
    obs_lists,
    loc_weight,
    send_rows,
    ocean_src,
    ocean_frac,
    ocean_ens,
):
    tile_obs = obs_pert.shape[1]
    extra = jnp.zeros((16, tile_obs), jnp.bfloat16).at[0].set(innovation).at[1].set(obs_prec)
    mixed = mixed_weights(
        send_rows[0], ocean_src, ocean_frac, obs_lists, loc_weight, obs_pert, extra
    )
    mixed = mixed[:, :, : ocean_ens.shape[0]]
    return apply_weights(ocean_ens, mixed)


def solution(mesh):
    return jax.shard_map(
        shards,
        mesh=mesh,
        in_specs=(
            P("member", "space"),
            P("space"),
            P("space"),
            P("space", None),
            P("space", None),
            P("space", None, None),
            P("space", None),
            P("space"),
            P(None, "space", "member"),
        ),
        out_specs=P(None, "space", "member"),
        check_vma=False,
    )
```

```python
import functools

import jax
import jax.numpy as jnp
from jax import lax
from jax.experimental import pallas as pl
from jax.experimental.pallas import tpu as pltpu
from jax.sharding import PartitionSpec as P

ITERS = 12
LANES = 128
CHUNK = 512


def split(value):
    high = value.astype(jnp.bfloat16)
    low = (value - high.astype(jnp.float32)).astype(jnp.bfloat16)
    return high, low


def left_side(value):
    return jnp.concatenate(split(value), axis=1)


def right_side(value):
    pair = left_side(value)
    filler = jnp.zeros((LANES - pair.shape[0], pair.shape[1]), jnp.bfloat16)
    return jnp.concatenate([pair, filler, pair, filler], axis=0)


def halves(product):
    return product[:, :LANES] + product[:, LANES:]


def mm(lhs, rhs):
    return jnp.dot(lhs, rhs, preferred_element_type=jnp.float32)


MESH = pl.DeviceIdType.MESH


def remote(src, dst, send_sem, recv_sem, device):
    return pltpu.make_async_remote_copy(
        src_ref=src, dst_ref=dst, send_sem=send_sem, recv_sem=recv_sem,
        device_id=device, device_id_type=MESH,
    )


def letkf_kernel(
    group, ns, nm,
    send_ref, src_ref, frac_ref, lists_hbm, loc_hbm, pert_ref, extra_ref, out_ref,
    lists_ref, loc_ref, local_sem, pert_all, extra_all, loc_f32, dense, gram, root, inverse, pulled, scales,
    trans_out, trans_in, up_out, up_in, down_out, down_in, mixed,
    z_send, z_recv, near_send, near_recv, info_send, info_recv, t_send, t_recv,
    up_send, up_recv, down_send, down_recv,
):
    s = lax.axis_index("space")
    m = lax.axis_index("member")
    members = pert_ref.shape[0] * nm
    tile_obs = pert_ref.shape[1]
    tile_his = tile_obs // LANES
    group_len = lists_ref.shape[0] // nm
    take_lists = pltpu.make_async_copy(lists_hbm, lists_ref, local_sem.at[0])
    take_loc = pltpu.make_async_copy(loc_hbm, loc_ref, local_sem.at[1])
    take_pert = pltpu.make_async_copy(pert_ref, pert_all.at[1, m], local_sem.at[2])
    for copy in (take_lists, take_loc, take_pert):
        copy.start()
    oblocks = out_ref.shape[0]
    z_peers = [lax.rem(m + k, nm) for k in range(1, nm)]
    s_peers = [lax.rem(s + k, ns) for k in range(1, ns)]
    left, right = lax.rem(s + ns - 1, ns), lax.rem(s + 1, ns)

    barrier = pltpu.get_barrier_semaphore()
    for peer in z_peers:
        pl.semaphore_signal(barrier, inc=1, device_id=(s, peer), device_id_type=MESH)
    for peer in s_peers:
        pl.semaphore_signal(barrier, inc=1, device_id=(peer, m), device_id_type=MESH)
    pl.semaphore_wait(barrier, len(z_peers) + len(s_peers))

    def to_z(peer):
        return remote(pert_ref, pert_all.at[1, m], z_send.at[peer], z_recv.at[m], (s, peer))

    def from_z(peer):
        return remote(pert_ref, pert_all.at[1, peer], z_send.at[m], z_recv.at[peer], (s, peer))

    def near(side, owner, src):
        target = right if side == 0 else left
        return remote(
            src, pert_all.at[2 * side, owner], near_send.at[side, owner],
            near_recv.at[side, owner], (target, m),
        )

    def info(side):
        target = right if side == 0 else left
        return remote(
            extra_ref, extra_all.at[2 * side], info_send.at[side], info_recv.at[side], (target, m)
        )

    order = sorted(range(nm - 1), key=lambda k: abs(k + 1 - nm / 2))
    for k in order:
        to_z(z_peers[k]).start()
    for side in range(2):
        near(side, m, pert_ref).start()
        info(side).start()
    extra_all[1] = extra_ref[...]
    take_lists.wait()
    take_loc.wait()
    take_pert.wait()
    loc_f32[...] = loc_ref[...].astype(jnp.float32)

    his = dense.shape[1]
    lobs = lists_ref.shape[1]
    hi_iota = lax.broadcasted_iota(jnp.int32, (his, lobs), 0)
    lo_iota = lax.broadcasted_iota(jnp.int32, (LANES, lobs), 0)
    rows = lax.broadcasted_iota(jnp.int32, (members, LANES), 0)
    cols = lax.broadcasted_iota(jnp.int32, (members, LANES), 1)
    on_diag = rows == cols
    half3 = jnp.where(on_diag, 1.5, 0.0)
    per = CHUNK // LANES

    def spread_lists(first):
        for b in range(group):
            row = send_ref[m, first + b] + m * group_len
            spots = lists_ref[pl.ds(row, 1), :]
            taper = loc_f32[pl.ds(row, 1), :]
            high, low = lax.shift_right_logical(spots, 7), jnp.bitwise_and(spots, LANES - 1)
            hi_hot = jnp.where(hi_iota == high, taper, 0.0).astype(jnp.bfloat16)
            lo_hot = jnp.where(lo_iota == low, 1.0, 0.0).astype(jnp.bfloat16)
            dense[b] = lax.dot_general(
                hi_hot, lo_hot, (((1,), (1,)), ((), ())), preferred_element_type=jnp.float32
            )
        gram[...] = jnp.zeros_like(gram)

    def add_piece(piece):
        def chunk_step(c, carry):
            span = pl.ds(pl.multiple_of(c * CHUNK, CHUNK), CHUNK)
            wide = jnp.concatenate(
                [pert_all[piece, i, :, span].astype(jnp.float32) for i in range(nm)], axis=0
            )
            extra = extra_all[piece, :, span]
            cells = jnp.concatenate([wide.astype(jnp.bfloat16), extra], axis=0)
            wide = wide * extra.astype(jnp.float32)[1:2]
            contract = (((1,), (1,)), ((), ()))
            for b in range(group):
                parts = []
                for j in range(per):
                    weight = dense[b, pl.ds(piece * tile_his + c * per + j, 1), :]
                    parts.append(wide[:, j * LANES : (j + 1) * LANES] * weight)
                high, low = split(jnp.concatenate(parts, axis=1))
                gram[b, :, : cells.shape[0]] += lax.dot_general(
                    high, cells, contract, preferred_element_type=jnp.float32
                ) + lax.dot_general(low, cells, contract, preferred_element_type=jnp.float32)
            return carry

        lax.fori_loop(0, tile_obs // CHUNK, chunk_step, 0)

    def roots_and_weights(first):
        for b in range(group):
            both = gram[b]
            pulled[b] = jnp.sum(jnp.where(cols == members, both, 0.0), axis=1, keepdims=True)
            matrix = jnp.where(cols < members, both, 0.0) + jnp.where(on_diag, members - 1.0, 0.0)
            scale = jnp.sum(
                jnp.sum(jnp.where(on_diag, matrix, 0.0), axis=1, keepdims=True),
                axis=0, keepdims=True,
            )
            scales[b] = jnp.broadcast_to(scale, (1, LANES))
            start = matrix / scale
            correction = half3 - 0.5 * start
            root[b] = halves(mm(left_side(start), right_side(correction)))
            inverse[b] = correction

        def newton(step, carry):
            corrections, pairs = [], []
            filler = jnp.zeros((LANES - members, 2 * LANES), jnp.bfloat16)
            for b in range(group):
                r, z = left_side(root[b]), left_side(inverse[b])
                rhs = jnp.concatenate([r, filler, r, filler], axis=0)
                corrections.append(half3 - 0.5 * halves(mm(z, rhs)))
                pairs.append(jnp.concatenate([r, z], axis=0))
            for b in range(group):
                both = halves(mm(pairs[b], right_side(corrections[b])))
                root[b] = both[:members]
                inverse[b] = both[members:]
            return carry

        lax.fori_loop(0, ITERS - 1, newton, 0)
        for b in range(group):
            z = inverse[b]
            scale = scales[b]
            half_way = jnp.sum(z * pulled[b], axis=0, keepdims=True)
            mean_weight = jnp.sum(z * half_way, axis=1, keepdims=True) / scale[:, :1]
            trans = jnp.sqrt((members - 1.0) / scale) * z + mean_weight
            trans_out[first + b] = trans.astype(jnp.bfloat16)

    spread_lists(0)
    for k in order:
        peer = z_peers[k]
        from_z(peer).wait_recv()
        for side in range(2):
            near(side, peer, pert_all.at[1, peer]).start()
    add_piece(1)
    for side in range(2):
        info(side).wait()
        for i in range(nm):
            near(side, i, pert_all.at[1, i]).wait()
        add_piece(2 * side)
    for peer in z_peers:
        to_z(peer).wait_send()
    roots_and_weights(0)
    if ns > group:

        def more(g, carry):
            spread_lists(g * group)
            for piece in range(3):
                add_piece(piece)
            roots_and_weights(g * group)
            return carry

        lax.fori_loop(1, ns // group, more, 0)

    def to_tile(peer):
        return remote(trans_out.at[peer], trans_in.at[s], t_send.at[peer], t_recv.at[s], (peer, m))

    def from_tile(peer):
        return remote(trans_out.at[peer], trans_in.at[peer], t_send.at[peer], t_recv.at[peer], (peer, m))

    for peer in s_peers:
        to_tile(peer).start()
    trans_in[s] = trans_out[s]
    for peer in s_peers:
        from_tile(peer).wait_recv()

    def mix(o, carry):
        total = jnp.zeros((members, LANES), jnp.float32)
        one, two, frac = src_ref[0, o], src_ref[1, o], frac_ref[o]
        for i in range(ns):
            slot = m * ns + i
            weight = jnp.where(one == slot, 1.0 - frac, 0.0) + jnp.where(two == slot, frac, 0.0)
            total += weight * trans_in[i].astype(jnp.float32)
        mixed[o] = total
        return carry

    def up(o):
        return remote(
            up_out.at[o], up_in.at[o], up_send.at[o], up_recv.at[o], (s, lax.rem(m + 1, nm))
        )

    def down(o):
        return remote(
            down_out.at[o], down_in.at[o], down_send.at[o], down_recv.at[o],
            (s, lax.rem(m + nm - 1, nm)),
        )

    def first_hop(o, carry):
        mix(o, carry)

        @pl.when(m == 0)
        def _():
            up_out[o] = mixed[o].astype(jnp.bfloat16)
            up(o).start()

        @pl.when(m == nm - 1)
        def _():
            down_out[o] = mixed[o].astype(jnp.bfloat16)
            down(o).start()

        return carry

    lax.fori_loop(0, oblocks, first_hop, 0)

    def pass_up(o, carry):
        up(o).wait_recv()

        @pl.when(m < nm - 1)
        def _():
            up_out[o] = (mixed[o] + up_in[o].astype(jnp.float32)).astype(jnp.bfloat16)
            up(o).start()

        return carry

    def pass_down(o, carry):
        down(o).wait_recv()

        @pl.when(m > 0)
        def _():
            down_out[o] = (mixed[o] + down_in[o].astype(jnp.float32)).astype(jnp.bfloat16)
            down(o).start()

        return carry

    lower = m < nm // 2

    @pl.when(jnp.logical_and(lower, m > 0))
    def _():
        lax.fori_loop(0, oblocks, pass_up, 0)

    @pl.when(m < nm - 1)
    def _():
        lax.fori_loop(0, oblocks, pass_down, 0)

    @pl.when(jnp.logical_not(lower))
    def _():
        lax.fori_loop(0, oblocks, pass_up, 0)

    def finish(o, carry):
        @pl.when(m == 0)
        def _():
            out_ref[o] = (mixed[o] + down_in[o].astype(jnp.float32)).astype(jnp.bfloat16)

        @pl.when(m == nm - 1)
        def _():
            out_ref[o] = (mixed[o] + up_in[o].astype(jnp.float32)).astype(jnp.bfloat16)

        @pl.when(jnp.logical_and(m > 0, m < nm - 1))
        def _():
            both = up_in[o].astype(jnp.float32) + down_in[o].astype(jnp.float32)
            out_ref[o] = (mixed[o] + both).astype(jnp.bfloat16)

        return carry

    lax.fori_loop(0, oblocks, finish, 0)

    def drain(o, carry):
        @pl.when(m < nm - 1)
        def _():
            up(o).wait_send()

        @pl.when(m > 0)
        def _():
            down(o).wait_send()

        return carry

    lax.fori_loop(0, oblocks, drain, 0)
    for peer in s_peers:
        to_tile(peer).wait_send()


def mixed_weights(send, src, frac, lists, loc, pert, extra):
    ns, nm = lax.axis_size("space"), lax.axis_size("member")
    shard, tile_obs = pert.shape
    members = shard * nm
    group = 8 if ns % 8 == 0 else ns
    oblocks = src.shape[1]
    his = 3 * tile_obs // LANES
    vmem = pl.BlockSpec(memory_space=pltpu.VMEM)
    hbm = pl.BlockSpec(memory_space=pl.ANY)
    smem = pl.BlockSpec(memory_space=pltpu.SMEM)
    dma = pltpu.SemaphoreType.DMA
    blocks = lambda n, kind: pltpu.VMEM((n, members, LANES), kind)
    return pl.pallas_call(
        functools.partial(letkf_kernel, group, ns, nm),
        in_specs=[smem, smem, smem, hbm, hbm, hbm, vmem],
        out_specs=vmem,
        out_shape=jax.ShapeDtypeStruct((oblocks, members, LANES), jnp.bfloat16),
        scratch_shapes=[
            pltpu.VMEM(lists.shape, lists.dtype),
            pltpu.VMEM(loc.shape, loc.dtype),
            dma((3,)),
            pltpu.VMEM((3, nm, shard, tile_obs), jnp.bfloat16),
            pltpu.VMEM((3,) + extra.shape, jnp.bfloat16),
            pltpu.VMEM(loc.shape, jnp.float32),
            pltpu.VMEM((group, his, LANES), jnp.float32),
            blocks(group, jnp.float32),
            blocks(group, jnp.float32),
            blocks(group, jnp.float32),
            pltpu.VMEM((group, members, 1), jnp.float32),
            pltpu.VMEM((group, 1, LANES), jnp.float32),
            blocks(ns, jnp.bfloat16),
            blocks(ns, jnp.bfloat16),
            blocks(oblocks, jnp.bfloat16),
            blocks(oblocks, jnp.bfloat16),
            blocks(oblocks, jnp.bfloat16),
            blocks(oblocks, jnp.bfloat16),
            blocks(oblocks, jnp.float32),
            dma((nm,)), dma((nm,)), dma((2, nm)), dma((2, nm)), dma((2,)), dma((2,)),
            dma((ns,)), dma((ns,)),
            dma((oblocks,)), dma((oblocks,)), dma((oblocks,)), dma((oblocks,)),
        ],
        compiler_params=pltpu.CompilerParams(collective_id=0, has_side_effects=True),
        name="mixed_weights",
    )(send, src, frac, lists, loc, pert, extra)


def apply_weights(ensemble, mixed):
    ens_mean = jnp.mean(ensemble, axis=0, dtype=jnp.float32)
    deviation = (ensemble.astype(jnp.float32) - ens_mean[None]).astype(jnp.bfloat16)
    product = jnp.einsum("jol,oji->iol", deviation, mixed, preferred_element_type=jnp.float32)
    return (ens_mean[None] + product).astype(jnp.bfloat16)


def shards(
    obs_pert,
    innovation,
    obs_prec,
    obs_lists,
    loc_weight,
    send_rows,
    ocean_src,
    ocean_frac,
    ocean_ens,
):
    tile_obs = obs_pert.shape[1]
    extra = jnp.zeros((16, tile_obs), jnp.bfloat16).at[0].set(innovation).at[1].set(obs_prec)
    mixed = mixed_weights(
        send_rows[0], ocean_src.T, ocean_frac, obs_lists, loc_weight, obs_pert, extra
    )
    mixed = mixed[:, :, : ocean_ens.shape[0]]
    return apply_weights(ocean_ens, mixed)


def solution(mesh):
    return jax.shard_map(
        shards,
        mesh=mesh,
        in_specs=(
            P("member", "space"),
            P("space"),
            P("space"),
            P("space", None),
            P("space", None),
            P("space", None, None),
            P("space", None),
            P("space"),
            P(None, "space", "member"),
        ),
        out_specs=P(None, "space", "member"),
        check_vma=False,
    )
```
